32 devices in a mesh: layer: 4 (over z), row: 2 (over x), col: 4 (over y, core).
Axes of the slice: x: 2, y: 2, z: 4, core: 2. Of those that a mesh axis runs over, the one named last changes fastest.
Arguments:
- cost_vector: float32 [8, 1024, 512], P('layer', 'row', 'col'), may hold values from -12 to 12
- metal_density: float32 [8, 1024, 512], P('layer', 'row', 'col'), may hold values from 0 to 0.5
- cap_class: int32 [8, 1024, 512], P('layer', 'row', 'col'), may hold values from 0 to 7
- blocked_mask: int32 [8, 1024, 512], P('layer', 'row', 'col'), may hold values 0 or 1
- fill_start: float32 [8, 1024, 512], P('layer', 'row', 'col'), may hold values from 0 to 1
- window_dual: float32 [8, 1024, 512], P('layer', 'row', 'col'), may hold values from -4 to 4
- layer_dual: float32 [8, 1024, 512], P('layer', 'row', 'col'), may hold values from -4 to 4
Outputs:
- fill_level: float32 [8, 1024, 512], P('layer', 'row', 'col')
- window_price: float32 [8, 1024, 512], P('layer', 'row', 'col')
- layer_price: float32 [8, 1024, 512], P('layer', 'row', 'col')
- primal_weight: float32 [], replicated
The draws below stay inside these ranges and needn't reach their ends.
All inputs are finite; a program needn't handle non-finite values. No bound on the sum of `blocked_mask` on one device may be relied on, other than what follows from the above.
Results may differ from the reference program's by a relative error of at most 0.00011.
Values sent between devices are 32-bit elements; how exact they have to be, the bound alone decides.
A program may use at most 64 MiB of HBM per device.

```python
import jax
import jax.numpy as jnp
from jax import lax

WIN = 50
CAP_LEVELS = 8
ITERS = 3
LAYERS = 8
ROWS = 1024
COLS = 512


def draw_cost_vector(key, part):
    first_key = jax.random.fold_in(key, 0)
    layer_pos = jnp.arange(LAYERS, dtype=jnp.float32)[:, None, None] / max(LAYERS - 1, 1)
    row_pos = jnp.arange(ROWS, dtype=jnp.float32)[None, :, None] / (ROWS - 1)
    col_pos = jnp.arange(COLS, dtype=jnp.float32)[None, None, :] / (COLS - 1)
    ramp_scale = 1.0 + 2.0 * (layer_pos + row_pos + col_pos) / 3.0
    base_draw = jax.random.normal(first_key, (LAYERS, ROWS, COLS), jnp.float32)
    return jnp.clip(base_draw * ramp_scale, -12.0, 12.0)


def touch_ends(array, own_key, least, largest):
    place = [jax.random.randint(jax.random.fold_in(own_key, axis), (), 0, length) for axis, length in enumerate(array.shape)]
    longest = array.shape.index(max(array.shape))
    beside = place[:longest] + [(place[longest] + 1) % array.shape[longest]] + place[longest + 1:]
    return array.at[tuple(place)].set(least).at[tuple(beside)].set(largest)


def block_scale(stream_key, shape, pieces, low, high):
    loudness = 1.0
    for axis_at, shards_of in pieces:
        draws = jax.random.uniform(jax.random.fold_in(jax.random.fold_in(stream_key, 6), axis_at), (shards_of,), jnp.float32, low / len(pieces), high / len(pieces))
        loudness = loudness * jnp.repeat(jnp.exp(draws), shape[axis_at] // shards_of).reshape((-1,) + (1,) * (len(shape) - 1 - axis_at))
    return loudness


def gaussian(key, dims, spread, reach, shards=(), held_as=jnp.bfloat16):
    result = spread * jax.random.normal(key, dims, jnp.float32)
    if shards:
        result = result * block_scale(key, dims, shards, -0.22, 0.18)
    return jnp.clip(result, -reach, reach).astype(held_as)


def setup_inputs(seed: int = 0) -> dict:
    key_of = jax.random.split(jax.random.key(seed), 8)
    return {
        "cost_vector": draw_cost_vector(jax.random.fold_in(key_of[7], 71), 0),
        "metal_density": jnp.clip(0.5 * jax.random.uniform(key_of[1], (LAYERS, ROWS, COLS), jnp.float32) ** block_scale(key_of[1], (LAYERS, ROWS, COLS), ((0, 4), (1, 2), (2, 4)), -0.2, 0.2), 0.0, 0.5),
        "cap_class": touch_ends(jax.random.randint(key_of[2], (LAYERS, ROWS, COLS), 0, CAP_LEVELS), jax.random.fold_in(key_of[2], 1), 0, CAP_LEVELS - 1).astype(jnp.int32),
        "blocked_mask": touch_ends((jax.random.randint(key_of[3], (LAYERS, ROWS, COLS), 0, 8) < 1).astype(jnp.int32), jax.random.fold_in(key_of[3], 1), 0, 1),
        "fill_start": jnp.clip(1.0 * jax.random.uniform(key_of[4], (LAYERS, ROWS, COLS), jnp.float32) ** block_scale(key_of[4], (LAYERS, ROWS, COLS), ((0, 4), (1, 2), (2, 4)), -0.2, 0.2), 0.0, 1.0),
        "window_dual": gaussian(key_of[5], (LAYERS, ROWS, COLS), 0.5, 4.0, ((0, 4), (1, 2), (2, 4)), jnp.float32),
        "layer_dual": gaussian(key_of[6], (LAYERS, ROWS, COLS), 0.5, 4.0, ((0, 4), (1, 2), (2, 4)), jnp.float32),
    }


step_eta = 0.4
low_density = 0.35
high_density = 0.65
layer_gap = 0.15
tiny_term = 1e-06

def window_sum(field, direction, start):
    extent = field.shape[direction]
    widths = [(0, 0), (0, 0), (0, 0)]
    widths[direction] = (WIN + 1, WIN)
    running = jnp.cumsum(jnp.pad(field, widths), axis=direction)
    upper_sum = lax.slice_in_dim(running, start + 2 * WIN, start + 2 * WIN + extent, axis=direction)
    lower_sum = lax.slice_in_dim(running, start + WIN, start + WIN + extent, axis=direction)
    return upper_sum - lower_sum

def box_sum(field, start):
    return window_sum(window_sum(field, 1, start), 2, start)

def reference(cost_vector, metal_density, cap_class, blocked_mask, fill_start, window_dual, layer_dual):
    layer_count = fill_start.shape[0]
    half_window = WIN // 2
    inverse_area = 1.0 / (WIN * WIN)
    keep_mask = (jnp.arange(layer_count) < layer_count - 1).astype(jnp.float32)[:, None, None]
    capacity = jnp.where(blocked_mask == 1, 0.0, (cap_class + 1).astype(jnp.float32) / CAP_LEVELS)
    has_floor = blocked_mask == 0
    filling = fill_start
    density_dual = window_dual
    stacked_dual = layer_dual * keep_mask
    weight = jnp.float32(1.0)
    for iteration in range(ITERS):
        primal_step = step_eta / weight
        dual_step = step_eta * weight
        earlier = jnp.concatenate([jnp.zeros_like(stacked_dual[:1]), stacked_dual[:-1]], axis=0)
        gradient = cost_vector + box_sum(density_dual, -(WIN - 1 - half_window)) * inverse_area + (stacked_dual - earlier)
        fill_new = jnp.clip(filling - primal_step * gradient, 0.0, capacity)
        moved = fill_new - filling
        level = fill_new + moved + metal_density
        later = jnp.concatenate([level[1:], jnp.zeros_like(level[:1])], axis=0)
        window_term = density_dual / dual_step + box_sum(level, -half_window) * inverse_area
        capped = jnp.minimum(window_term, high_density)
        clipped = jnp.where(has_floor, jnp.maximum(capped, low_density), capped)
        density_new = dual_step * (window_term - clipped)
        layer_term = stacked_dual / dual_step + keep_mask * (level - later)
        stacked_new = dual_step * (layer_term - jnp.clip(layer_term, -layer_gap, layer_gap)) * keep_mask
        primal_sum = jnp.sum(moved * moved)
        dual_sum = jnp.sum((density_new - density_dual) ** 2) + jnp.sum((stacked_new - stacked_dual) ** 2)
        weight = jnp.sqrt(weight) * jnp.sqrt(jnp.sqrt((dual_sum + tiny_term) / (primal_sum + tiny_term)))
        filling = fill_new
        density_dual = density_new
        stacked_dual = stacked_new
    return (filling, density_dual, stacked_dual, weight)
```

```python
import functools

import jax
import jax.numpy as jnp
from jax import lax
from jax.experimental import pallas as pl
from jax.experimental.pallas import tpu as pltpu
from jax.sharding import PartitionSpec as P

WIN = 50
CAP_LEVELS = 8
ITERS = 3

step_eta = 0.4
low_density = 0.35
high_density = 0.65
layer_gap = 0.15
tiny_term = 1e-06

HALF = WIN // 2
HALO = -(-HALF // 16) * 16
TILE = 128
MESH = pl.DeviceIdType.MESH
DIRS = ((-1, 0), (1, 0), (0, -1), (0, 1), (-1, -1), (-1, 1), (1, -1), (1, 1))
F32 = jnp.float32
BF16 = jnp.bfloat16
NT = (((1,), (1,)), ((), ()))
NN = (((1,), (0,)), ((), ()))


def split(value):
    high = value.astype(BF16)
    low = (value - high.astype(F32)).astype(BF16)
    return high, low


def dot(left, right, dims=NN):
    return lax.dot_general(left, right, dims, preferred_element_type=F32)


def iota(shape, dim):
    return lax.broadcasted_iota(jnp.int32, shape, dim)


def window(offset, start):
    return jnp.where((offset >= start) & (offset < start + WIN), 1.0, 0.0).astype(BF16)


def kernel(
    sizes, cost, dens, capc, blocked, x_in, y_in, z_in,
    x, y_out, z, weight_out,
    ext_u, ext_y, et_u, et_y, ht_u, ht_y, above, below, zlow, cap, grad,
    band_r, band_h, band_c, band_d, pick, slots,
    send_sem, recv_sem, zsend, zrecv, ssend, srecv,
):
    nl, nr, nc = sizes
    layers, rows, cols = x_in.shape
    ndev = nl * nr * nc
    il, ir, ic = lax.axis_index("layer"), lax.axis_index("row"), lax.axis_index("col")
    me = (il * nr + ir) * nc + ic
    tiles = rows // TILE
    inverse_area = 1.0 / (WIN * WIN)
    own = pl.ds(HALO, rows)

    for ref in (ext_u, ext_y):
        ref[:, :HALO, :] = jnp.zeros((layers, HALO, cols), F32)
        ref[:, HALO + rows :, :] = jnp.zeros((layers, HALO, cols), F32)
    for ref in (ht_u, ht_y, above, below, zlow):
        ref[...] = jnp.zeros(ref.shape, F32)

    barrier = pltpu.get_barrier_semaphore()

    def greet(i, _):
        @pl.when(i != me)
        def _():
            pl.semaphore_signal(
                barrier, inc=1, device_id=(i // (nr * nc), (i // nc) % nr, i % nc),
                device_id_type=MESH,
            )
        return 0

    lax.fori_loop(0, ndev, greet, 0)

    keep_top = jnp.where(il < nl - 1, 1.0, 0.0).astype(F32)
    keep_low = jnp.where(il > 0, 1.0, 0.0).astype(F32)
    for which, start in ((0, -HALF), (1, 1 - HALF)):
        shape = (TILE, TILE + 2 * HALO)
        band_r[which] = window(iota(shape, 1) - HALO - iota(shape, 0), start)
        shape = (TILE, 3 * TILE)
        band_h[which] = window(iota(shape, 1) - TILE - iota(shape, 0), start)
        shape = (cols, cols)
        band_c[which] = window(iota(shape, 0) - iota(shape, 1), start)
        shape = (2 * HALO, cols)
        k = iota(shape, 0)
        place = jnp.where(k < HALO, k - HALO, k - HALO + cols)
        band_d[which] = window(place - iota(shape, 1), start)
    shape = (2 * HALO, cols)
    k = iota(shape, 0)
    place = jnp.where(k < HALO, k, k - 2 * HALO + cols)
    pick[...] = jnp.where(place == iota(shape, 1), 1.0, 0.0).astype(BF16)

    def span(t, base=0):
        return pl.ds(pl.multiple_of(t * TILE + base, 16), TILE)

    def lanes(t):
        return pl.ds(pl.multiple_of(t * TILE, TILE), TILE)

    def put_edges(et, l, t, value):
        high, low = split(value)
        et[l, :, lanes(t)] = dot(pick[...], high, NT) + dot(pick[...], low, NT)

    def prepare(t, _):
        for l in range(layers):
            value = y_in[l, span(t), :]
            ext_y[l, span(t, HALO), :] = value
            put_edges(et_y, l, t, value)
        return 0

    lax.fori_loop(0, tiles, prepare, 0)

    pl.semaphore_wait(barrier, ndev - 1)

    def copies(field):
        ext, et, ht = ((ext_u, et_u, ht_u), (ext_y, et_y, ht_y))[field]
        result = []
        for d, (dr, dc) in enumerate(DIRS):
            if dc == 0:
                src = ext.at[:, pl.ds(HALO if dr < 0 else rows, HALO), :]
                dst = ext.at[:, pl.ds(HALO + rows if dr < 0 else 0, HALO), :]
            else:
                from_rows = pl.ds(0 if dc < 0 else HALO, HALO)
                to_rows = pl.ds(HALO if dc < 0 else 0, HALO)
                if dr == 0:
                    src, dst = et.at[:, from_rows, :], ht.at[:, to_rows, pl.ds(TILE, rows)]
                elif dr < 0:
                    src = et.at[:, from_rows, pl.ds(0, TILE)]
                    dst = ht.at[:, to_rows, pl.ds(TILE + rows, TILE)]
                else:
                    src = et.at[:, from_rows, pl.ds(rows - TILE, TILE)]
                    dst = ht.at[:, to_rows, pl.ds(0, TILE)]
            to, frm = [], []
            if dr < 0:
                to.append(ir > 0)
                frm.append(ir < nr - 1)
            if dr > 0:
                to.append(ir < nr - 1)
                frm.append(ir > 0)
            if dc < 0:
                to.append(ic > 0)
                frm.append(ic < nc - 1)
            if dc > 0:
                to.append(ic < nc - 1)
                frm.append(ic > 0)
            copy = pltpu.make_async_remote_copy(
                src_ref=src, dst_ref=dst, send_sem=send_sem.at[field, d],
                recv_sem=recv_sem.at[field, d],
                device_id=(il, ir + dr, ic + dc), device_id_type=MESH,
            )
            result.append(
                (copy, functools.reduce(jnp.logical_and, to), functools.reduce(jnp.logical_and, frm))
            )
        return result

    halo_copies = (copies(0), copies(1))

    def begin(field, which):
        for d in which:
            copy, to, _ = halo_copies[field][d]
            pl.when(to)(copy.start)

    def finish(field):
        for copy, to, frm in halo_copies[field]:
            pl.when(frm)(copy.wait_recv)
            pl.when(to)(copy.wait_send)

    def up(src, dst, which=0):
        return pltpu.make_async_remote_copy(
            src_ref=src, dst_ref=dst, send_sem=zsend.at[which], recv_sem=zrecv.at[which],
            device_id=(il + 1, ir, ic), device_id_type=MESH,
        )

    def down(src, dst):
        return pltpu.make_async_remote_copy(
            src_ref=src, dst_ref=dst, send_sem=zsend.at[1], recv_sem=zrecv.at[1],
            device_id=(il - 1, ir, ic), device_id_type=MESH,
        )

    has_above, has_below = il < nl - 1, il > 0
    begin(1, (4, 5, 6, 7, 2, 3, 0, 1))
    first_up = up(z_in.at[layers - 1], zlow, 2)
    pl.when(has_above)(first_up.start)

    def begin_state(t, _):
        for l in range(layers):
            at = (l, span(t), slice(None))
            x[at] = x_in[at]
            z[at] = z_in[at] * keep_top if l == layers - 1 else z_in[at]
            level = (capc[at] + 1).astype(F32) * (1.0 / CAP_LEVELS)
            cap[at] = jnp.where(blocked[at] == 1, 0.0, level)
        return 0

    lax.fori_loop(0, tiles, begin_state, 0)

    def box(ext, ht, which, l, t):
        tall = pl.ds(pl.multiple_of(t * TILE, TILE), TILE + 2 * HALO)
        high, low = split(ext[l, tall, :])
        band = band_r[which]
        mid = dot(band, high) + dot(band, low)
        high, low = split(ht[l, :, pl.ds(pl.multiple_of(t * TILE, TILE), 3 * TILE)])
        band = band_h[which]
        side = dot(band, high, NT) + dot(band, low, NT)
        mid_high, mid_low = split(mid)
        side_high, side_low = split(side)
        return (
            dot(mid_high, band_c[which]) + dot(mid_low, band_c[which])
            + dot(side_high, band_d[which]) + dot(side_low, band_d[which])
        )

    def fold(value):
        return jnp.sum((value * value).reshape(TILE // 8, 8, cols), axis=0)

    none = jnp.zeros((8, cols), F32)
    weight = jnp.ones((1, cols), F32)
    for step in range(ITERS):
        last = step == ITERS - 1
        finish(1)

        def gradient(t, _):
            for l in range(layers):
                at = (l, span(t), slice(None))
                grad[at] = cost[at] + box(ext_y, ht_y, 1, l, t) * inverse_area
            return 0

        lax.fori_loop(0, tiles, gradient, 0)
        if step == 0:
            pl.when(has_below)(first_up.wait_recv)
            pl.when(has_above)(first_up.wait_send)
        else:
            sums_done()
            both = jnp.sum(slots[step - 1], axis=0)
            primal = jnp.sum(both[0:1], axis=1, keepdims=True)
            dual = jnp.sum(both[1:2], axis=1, keepdims=True)
            ratio = jnp.broadcast_to((dual + tiny_term) / (primal + tiny_term), (1, cols))
            weight = jnp.sqrt(weight) * jnp.sqrt(jnp.sqrt(ratio))
        tau = step_eta / weight
        sigma = step_eta * weight
        sigma_inverse = 1.0 / sigma

        def primal_move(t, total):
            for l in range(layers):
                at = (l, span(t), slice(None))
                earlier = zlow[span(t), :] if l == 0 else z[l - 1, span(t), :]
                old = x[at]
                new = jnp.minimum(
                    jnp.maximum(old - tau * (grad[at] + (z[at] - earlier)), 0.0), cap[at]
                )
                moved = new - old
                x[at] = new
                total = total + fold(moved)
                value = new + moved + dens[at]
                ext_u[l, span(t, HALO), :] = value
                put_edges(et_u, l, t, value)
            return total

        primal_sum = lax.fori_loop(0, tiles, primal_move, none)
        begin(0, (4, 5, 6, 7, 2, 3, 0, 1))
        send_down = down(ext_u.at[0, own, :], above)
        if not last:
            send_up = up(ext_u.at[layers - 1, own, :], below)
            pl.when(has_above)(send_up.start)
        pl.when(has_below)(send_down.start)
        finish(0)

        def dual_move(t, total):
            for l in range(layers):
                at = (l, span(t), slice(None))
                old = ext_y[l, span(t, HALO), :]
                term = old * sigma_inverse + box(ext_u, ht_u, 0, l, t) * inverse_area
                capped = jnp.minimum(term, high_density)
                clipped = jnp.where(
                    blocked[at] == 0, jnp.maximum(capped, low_density), capped
                )
                new = sigma * (term - clipped)
                total = total + fold(new - old)
                if last:
                    y_out[at] = new
                else:
                    ext_y[l, span(t, HALO), :] = new
                    put_edges(et_y, l, t, new)
            return total

        dual_sum = lax.fori_loop(0, tiles, dual_move, none)
        if not last:
            begin(1, (4, 5, 6, 7, 2, 3, 0, 1))

        pl.when(has_above)(send_down.wait_recv)
        pl.when(has_below)(send_down.wait_send)
        if not last:
            pl.when(has_below)(send_up.wait_recv)
            pl.when(has_above)(send_up.wait_send)

        def layer_move(t, total):
            def update(old, here, later, keep):
                term = old * sigma_inverse + keep * (here - later)
                return sigma * (term - jnp.clip(term, -layer_gap, layer_gap)) * keep

            levels = [ext_u[l, span(t, HALO), :] for l in range(layers)] + [above[span(t), :]]
            for l in range(layers):
                at = (l, span(t), slice(None))
                old = z[at]
                new = update(old, levels[l], levels[l + 1], keep_top if l == layers - 1 else 1.0)
                z[at] = new
                total = total + fold(new - old)
            if not last:
                zlow[span(t), :] = update(zlow[span(t), :], below[span(t), :], levels[0], keep_low)
            return total

        dual_sum = lax.fori_loop(0, tiles, layer_move, dual_sum)
        slots[step, pl.ds(me, 1)] = jnp.concatenate(
            [jnp.sum(primal_sum, axis=0, keepdims=True), jnp.sum(dual_sum, axis=0, keepdims=True)],
            axis=0,
        )[None]

        def tell(i, _, step=step):
            @pl.when(i != me)
            def _():
                pltpu.make_async_remote_copy(
                    src_ref=slots.at[step, me], dst_ref=slots.at[step, me],
                    send_sem=ssend.at[step], recv_sem=srecv.at[step],
                    device_id=(i // (nr * nc), (i // nc) % nr, i % nc), device_id_type=MESH,
                ).start()
            return 0

        lax.fori_loop(0, ndev, tell, 0)

        def sums_done(step=step):
            some = slots.at[step, pl.ds(0, ndev - 1)]
            pltpu.make_async_copy(some, some, srecv.at[step]).wait()
            pltpu.make_async_copy(some, some, ssend.at[step]).wait()

    sums_done()
    both = jnp.sum(slots[ITERS - 1], axis=0)
    primal = jnp.sum(both[0:1], axis=1, keepdims=True)
    dual = jnp.sum(both[1:2], axis=1, keepdims=True)
    ratio = jnp.broadcast_to((dual + tiny_term) / (primal + tiny_term), (1, cols))
    weight_out[...] = jnp.sqrt(weight) * jnp.sqrt(jnp.sqrt(ratio))


def local(sizes, *args):
    layers, rows, cols = args[0].shape
    ndev = sizes[0] * sizes[1] * sizes[2]
    whole = jax.ShapeDtypeStruct((layers, rows, cols), F32)
    vmem = pl.BlockSpec(memory_space=pltpu.VMEM)
    ext = pltpu.VMEM((layers, rows + 2 * HALO, cols), F32)
    et = pltpu.VMEM((layers, 2 * HALO, rows), F32)
    ht = pltpu.VMEM((layers, 2 * HALO, rows + 2 * TILE), F32)
    plane = pltpu.VMEM((rows, cols), F32)
    full = pltpu.VMEM((layers, rows, cols), F32)
    x, y, z, weight = pl.pallas_call(
        functools.partial(kernel, sizes),
        out_shape=(whole, whole, whole, jax.ShapeDtypeStruct((1, cols), F32)),
        in_specs=[vmem] * 7,
        out_specs=(vmem,) * 4,
        scratch_shapes=[
            ext, ext, et, et, ht, ht, plane, plane, plane, full, full,
            pltpu.VMEM((2, TILE, TILE + 2 * HALO), BF16),
            pltpu.VMEM((2, TILE, 3 * TILE), BF16),
            pltpu.VMEM((2, cols, cols), BF16),
            pltpu.VMEM((2, 2 * HALO, cols), BF16),
            pltpu.VMEM((2 * HALO, cols), BF16),
            pltpu.VMEM((ITERS, ndev, 2, cols), F32),
            pltpu.SemaphoreType.DMA((2, 8)),
            pltpu.SemaphoreType.DMA((2, 8)),
            pltpu.SemaphoreType.DMA((3,)),
            pltpu.SemaphoreType.DMA((3,)),
            pltpu.SemaphoreType.DMA((ITERS,)),
            pltpu.SemaphoreType.DMA((ITERS,)),
        ],
        compiler_params=pltpu.CompilerParams(collective_id=0, has_side_effects=True),
        name="fill_steps",
    )(*args)
    return x, y, z, weight[0, 0]


def solution(mesh):
    sizes = tuple(mesh.shape[axis] for axis in ("layer", "row", "col"))
    spec = P("layer", "row", "col")
    return jax.shard_map(
        functools.partial(local, sizes),
        mesh=mesh,
        in_specs=(spec,) * 7,
        out_specs=(spec, spec, spec, P()),
        check_vma=False,
    )
```

```python
import functools

import jax
import jax.numpy as jnp
from jax import lax
from jax.experimental import pallas as pl
from jax.experimental.pallas import tpu as pltpu
from jax.sharding import PartitionSpec as P

WIN = 50
CAP_LEVELS = 8
ITERS = 3

step_eta = 0.4
low_density = 0.35
high_density = 0.65
layer_gap = 0.15
tiny_term = 1e-06

HALF = WIN // 2
HALO = -(-HALF // 16) * 16
TILE = 128
MESH = pl.DeviceIdType.MESH
DIRS = ((-1, 0), (1, 0), (0, -1), (0, 1), (-1, -1), (-1, 1), (1, -1), (1, 1))
F32 = jnp.float32
BF16 = jnp.bfloat16
NT = (((1,), (1,)), ((), ()))
NN = (((1,), (0,)), ((), ()))


def split(value):
    high = value.astype(BF16)
    low = (value - high.astype(F32)).astype(BF16)
    return high, low


def dot(left, right, dims=NN):
    return lax.dot_general(left, right, dims, preferred_element_type=F32)


def iota(shape, dim):
    return lax.broadcasted_iota(jnp.int32, shape, dim)


def window(offset, start):
    return jnp.where((offset >= start) & (offset < start + WIN), 1.0, 0.0).astype(BF16)


def kernel(
    sizes, cost_in, dens_in, capc_in, blocked_in, x_in, y_in, z_in,
    x, y_out, z, weight_out,
    cost, dens, capc, blocked,
    ext_u, ext_y, et_u, et_y, ht_u, ht_y, above, below, zlow, cap, grad,
    band_r, band_h, band_c, band_d, pick, plane_slots, layer_slots,
    load_sem, send_sem, recv_sem, first_sem, zsend, zrecv, sum_sem,
):
    nl, nr, nc = sizes
    layers, rows, cols = x_in.shape
    peers = nr * nc
    il, ir, ic = lax.axis_index("layer"), lax.axis_index("row"), lax.axis_index("col")
    me = ir * nc + ic
    tiles = rows // TILE
    order = list(dict.fromkeys((0, tiles - 1, *range(tiles))))
    inverse_area = 1.0 / (WIN * WIN)
    own = pl.ds(HALO, rows)

    pairs = (
        (y_in, ext_y.at[:, own, :]), (x_in, x), (z_in, z), (cost_in, cost), (capc_in, capc),
        (blocked_in, blocked), (dens_in, dens),
    )
    loads = [pltpu.make_async_copy(a, b, load_sem.at[n]) for n, (a, b) in enumerate(pairs)]
    for load in loads:
        load.start()

    for ref in (ext_u, ext_y):
        ref[:, :HALO, :] = jnp.zeros((layers, HALO, cols), F32)
        ref[:, HALO + rows :, :] = jnp.zeros((layers, HALO, cols), F32)
    for ref in (ht_u, ht_y, above, below, zlow):
        ref[...] = jnp.zeros(ref.shape, F32)

    barrier = pltpu.get_barrier_semaphore()

    def in_plane(act):
        def one(i, _):
            pl.when(i != me)(lambda: act((il, i // nc, i % nc)))
            return 0

        lax.fori_loop(0, peers, one, 0, unroll=peers <= 16)

    def in_stack(act):
        for i in range(nl):
            pl.when(i != il)(lambda i=i: act((i, ir, ic)))

    def greet(device):
        pl.semaphore_signal(barrier, inc=1, device_id=device, device_id_type=MESH)

    in_plane(greet)
    in_stack(greet)

    keep_top = jnp.where(il < nl - 1, 1.0, 0.0).astype(F32)
    keep_low = jnp.where(il > 0, 1.0, 0.0).astype(F32)
    for which, start in ((0, -HALF), (1, 1 - HALF)):
        shape = (TILE, TILE + 2 * HALO)
        band_r[which] = window(iota(shape, 1) - HALO - iota(shape, 0), start)
        shape = (TILE, 3 * TILE)
        band_h[which] = window(iota(shape, 1) - TILE - iota(shape, 0), start)
        shape = (cols, cols)
        band_c[which] = window(iota(shape, 0) - iota(shape, 1), start)
        shape = (2 * HALO, cols)
        k = iota(shape, 0)
        place = jnp.where(k < HALO, k - HALO, k - HALO + cols)
        band_d[which] = window(place - iota(shape, 1), start)
    shape = (2 * HALO, cols)
    k = iota(shape, 0)
    place = jnp.where(k < HALO, k, k - 2 * HALO + cols)
    pick[...] = jnp.where(place == iota(shape, 1), 1.0, 0.0).astype(BF16)

    def span(t, base=0):
        return pl.ds(t * TILE + base, TILE)

    def put_edges(et, l, t, value):
        high, low = split(value)
        et[l, :, span(t)] = dot(pick[...], high, NT) + dot(pick[...], low, NT)

    loads[0].wait()
    for t in range(tiles):
        for l in range(layers):
            put_edges(et_y, l, t, ext_y[l, span(t, HALO), :])

    pl.semaphore_wait(barrier, peers - 1 + nl - 1)

    def copies(field):
        ext, et, ht = ((ext_u, et_u, ht_u), (ext_y, et_y, ht_y))[field]
        result = []
        for d, (dr, dc) in enumerate(DIRS):
            if dc == 0:
                src = ext.at[:, pl.ds(HALO if dr < 0 else rows, HALO), :]
                dst = ext.at[:, pl.ds(HALO + rows if dr < 0 else 0, HALO), :]
            else:
                from_rows = pl.ds(0 if dc < 0 else HALO, HALO)
                to_rows = pl.ds(HALO if dc < 0 else 0, HALO)
                if dr == 0:
                    src, dst = et.at[:, from_rows, :], ht.at[:, to_rows, pl.ds(TILE, rows)]
                elif dr < 0:
                    src = et.at[:, from_rows, pl.ds(0, TILE)]
                    dst = ht.at[:, to_rows, pl.ds(TILE + rows, TILE)]
                else:
                    src = et.at[:, from_rows, pl.ds(rows - TILE, TILE)]
                    dst = ht.at[:, to_rows, pl.ds(0, TILE)]
            to, frm = [], []
            if dr < 0:
                to.append(ir > 0)
                frm.append(ir < nr - 1)
            if dr > 0:
                to.append(ir < nr - 1)
                frm.append(ir > 0)
            if dc < 0:
                to.append(ic > 0)
                frm.append(ic < nc - 1)
            if dc > 0:
                to.append(ic < nc - 1)
                frm.append(ic > 0)
            copy = pltpu.make_async_remote_copy(
                src_ref=src, dst_ref=dst, send_sem=send_sem.at[field, d],
                recv_sem=recv_sem.at[field, d],
                device_id=(il, ir + dr, ic + dc), device_id_type=MESH,
            )
            result.append(
                (copy, functools.reduce(jnp.logical_and, to), functools.reduce(jnp.logical_and, frm))
            )
        return result

    halo_copies = (copies(0), copies(1))

    def begin(field, which):
        for d in which:
            copy, to, _ = halo_copies[field][d]
            pl.when(to)(copy.start)

    def finish(field):
        for copy, to, frm in halo_copies[field]:
            pl.when(frm)(copy.wait_recv)
            pl.when(to)(copy.wait_send)

    has_above, has_below = il < nl - 1, il > 0
    EDGE, SIDE = (4, 5, 6, 7, 0, 1), (2, 3)
    begin(1, EDGE + SIDE)
    first_up = pltpu.make_async_remote_copy(
        src_ref=z_in.at[layers - 1], dst_ref=zlow, send_sem=first_sem.at[0],
        recv_sem=first_sem.at[1], device_id=(il + 1, ir, ic), device_id_type=MESH,
    )
    pl.when(has_above)(first_up.start)

    def up(t):
        return pltpu.make_async_remote_copy(
            src_ref=ext_u.at[layers - 1, span(t, HALO), :], dst_ref=below.at[span(t), :],
            send_sem=zsend.at[0, t], recv_sem=zrecv.at[0, t],
            device_id=(il + 1, ir, ic), device_id_type=MESH,
        )

    def down(t):
        return pltpu.make_async_remote_copy(
            src_ref=ext_u.at[0, span(t, HALO), :], dst_ref=above.at[span(t), :],
            send_sem=zsend.at[1, t], recv_sem=zrecv.at[1, t],
            device_id=(il - 1, ir, ic), device_id_type=MESH,
        )

    def inner(ext, which, l, t):
        first = HALO if t == 0 else 0
        end = TILE + HALO if t == tiles - 1 else TILE + 2 * HALO
        high, low = split(ext[l, t * TILE + first : t * TILE + end, :])
        band = band_r[which, :, first:end]
        high, low = split(dot(band, high) + dot(band, low))
        return dot(high, band_c[which]) + dot(low, band_c[which])

    def outer(ext, ht, which, l, t):
        high, low = split(ht[l, :, t * TILE : (t + 3) * TILE])
        band = band_h[which]
        high, low = split(dot(band, high, NT) + dot(band, low, NT))
        total = dot(high, band_d[which]) + dot(low, band_d[which])
        for edge, at, base in ((0, 0, 0), (tiles - 1, TILE + HALO, HALO + rows)):
            if t == edge:
                high, low = split(ext[l, base : base + HALO, :])
                band = band_r[which, :, at : at + HALO]
                high, low = split(dot(band, high) + dot(band, low))
                total = total + dot(high, band_c[which]) + dot(low, band_c[which])
        return total

    everywhere = [(l, t, (l, span(t), slice(None))) for t in order for l in range(layers)]
    for n in range(1, 7):
        loads[n].wait()
    z[layers - 1] = z[layers - 1] * keep_top
    for l, t, at in everywhere:
        level = (capc[at] + 1).astype(F32) * (1.0 / CAP_LEVELS)
        cap[at] = jnp.where(blocked[at] == 1, 0.0, level)

    def fold(value):
        return jnp.sum((value * value).reshape(TILE // 8, 8, cols), axis=0)

    def sum_copy(slots, step, mine, stage, device):
        return pltpu.make_async_remote_copy(
            src_ref=slots.at[step, mine], dst_ref=slots.at[step, mine],
            send_sem=sum_sem.at[stage, 0, step], recv_sem=sum_sem.at[stage, 1, step],
            device_id=device, device_id_type=MESH,
        )

    def sums_wait(slots, step, stage, count):
        if count > 1:
            some = slots.at[step, pl.ds(0, count - 1)]
            pltpu.make_async_copy(some, some, sum_sem.at[stage, 1, step]).wait()
            pltpu.make_async_copy(some, some, sum_sem.at[stage, 0, step]).wait()

    def sums_begin(step, primal_sum, dual_sum):
        plane_slots[step, pl.ds(me, 1)] = jnp.concatenate(
            [jnp.sum(primal_sum, axis=0, keepdims=True), jnp.sum(dual_sum, axis=0, keepdims=True)],
            axis=0,
        )[None]
        in_plane(lambda device: sum_copy(plane_slots, step, me, 0, device).start())

    def sums_forward(step):
        sums_wait(plane_slots, step, 0, peers)
        layer_slots[step, pl.ds(il, 1)] = jnp.sum(plane_slots[step], axis=0)[None]
        in_stack(lambda device: sum_copy(layer_slots, step, il, 1, device).start())

    def sums_end(step, weight):
        sums_wait(layer_slots, step, 1, nl)
        both = jnp.sum(layer_slots[step], axis=0)
        primal = jnp.sum(both[0:1], axis=1, keepdims=True)
        dual = jnp.sum(both[1:2], axis=1, keepdims=True)
        ratio = jnp.broadcast_to((dual + tiny_term) / (primal + tiny_term), (1, cols))
        return jnp.sqrt(weight) * jnp.sqrt(jnp.sqrt(ratio))

    weight = jnp.ones((1, cols), F32)
    for step in range(ITERS):
        last = step == ITERS - 1
        for l, t, at in everywhere:
            grad[at] = cost[at] + inner(ext_y, 1, l, t) * inverse_area
        if step > 0:
            sums_forward(step - 1)
        else:
            pl.when(has_below)(first_up.wait_recv)
            pl.when(has_above)(first_up.wait_send)
        finish(1)
        for l, t, at in everywhere:
            earlier = zlow[span(t), :] if l == 0 else z[l - 1, span(t), :]
            grad[at] = grad[at] + outer(ext_y, ht_y, 1, l, t) * inverse_area + (z[at] - earlier)
        if step > 0:
            weight = sums_end(step - 1, weight)
        tau = step_eta / weight
        sigma = step_eta * weight
        sigma_inverse = 1.0 / sigma

        primal_sum = jnp.zeros((8, cols), F32)
        for l, t, at in everywhere:
            old = x[at]
            new = jnp.minimum(jnp.maximum(old - tau * grad[at], 0.0), cap[at])
            moved = new - old
            x[at] = new
            primal_sum = primal_sum + fold(moved)
            value = new + moved + dens[at]
            ext_u[l, span(t, HALO), :] = value
            put_edges(et_u, l, t, value)
            if l == layers - 1:
                if not last:
                    pl.when(has_above)(up(t).start)
                pl.when(has_below)(down(t).start)
                if t == order[min(1, tiles - 1)]:
                    begin(0, EDGE)
        begin(0, SIDE)
        for l, t, at in everywhere:
            grad[at] = inner(ext_u, 0, l, t)
        finish(0)

        dual_sum = jnp.zeros((8, cols), F32)
        for l, t, at in everywhere:
            old = ext_y[l, span(t, HALO), :]
            term = old * sigma_inverse + (grad[at] + outer(ext_u, ht_u, 0, l, t)) * inverse_area
            capped = jnp.minimum(term, high_density)
            clipped = jnp.where(blocked[at] == 0, jnp.maximum(capped, low_density), capped)
            new = sigma * (term - clipped)
            dual_sum = dual_sum + fold(new - old)
            if last:
                y_out[at] = new
            else:
                ext_y[l, span(t, HALO), :] = new
                put_edges(et_y, l, t, new)
                if l == layers - 1 and t == order[min(1, tiles - 1)]:
                    begin(1, EDGE)
        if not last:
            begin(1, SIDE)

        def update(old, here, later, keep):
            term = old * sigma_inverse + keep * (here - later)
            return sigma * (term - jnp.clip(term, -layer_gap, layer_gap)) * keep

        for t in order:
            pl.when(has_above)(down(t).wait_recv)
            pl.when(has_below)(down(t).wait_send)
            if not last:
                pl.when(has_below)(up(t).wait_recv)
                pl.when(has_above)(up(t).wait_send)
            levels = [ext_u[l, span(t, HALO), :] for l in range(layers)] + [above[span(t), :]]
            for l in range(layers):
                at = (l, span(t), slice(None))
                old = z[at]
                new = update(old, levels[l], levels[l + 1], keep_top if l == layers - 1 else 1.0)
                z[at] = new
                dual_sum = dual_sum + fold(new - old)
            if not last:
                zlow[span(t), :] = update(zlow[span(t), :], below[span(t), :], levels[0], keep_low)
        sums_begin(step, primal_sum, dual_sum)

    sums_forward(ITERS - 1)
    weight_out[...] = sums_end(ITERS - 1, weight)


def local(sizes, *args):
    layers, rows, cols = args[0].shape
    peers = sizes[1] * sizes[2]
    tiles = rows // TILE
    whole = jax.ShapeDtypeStruct((layers, rows, cols), F32)
    vmem = pl.BlockSpec(memory_space=pltpu.VMEM)
    anywhere = pl.BlockSpec(memory_space=pl.ANY)
    full = pltpu.VMEM((layers, rows, cols), F32)
    full_int = pltpu.VMEM((layers, rows, cols), jnp.int32)
    line = pltpu.VMEM((1, cols), F32)
    ext = pltpu.VMEM((layers, rows + 2 * HALO, cols), F32)
    et = pltpu.VMEM((layers, 2 * HALO, rows), F32)
    ht = pltpu.VMEM((layers, 2 * HALO, rows + 2 * TILE), F32)
    plane = pltpu.VMEM((rows, cols), F32)
    x, y, z, weight = pl.pallas_call(
        functools.partial(kernel, sizes),
        out_shape=(full, full, full, line),
        in_specs=[anywhere] * 7,
        out_specs=(vmem,) * 4,
        scratch_shapes=[
            full, full, full_int, full_int,
            ext, ext, et, et, ht, ht, plane, plane, plane, full, full,
            pltpu.VMEM((2, TILE, TILE + 2 * HALO), BF16),
            pltpu.VMEM((2, TILE, 3 * TILE), BF16),
            pltpu.VMEM((2, cols, cols), BF16),
            pltpu.VMEM((2, 2 * HALO, cols), BF16),
            pltpu.VMEM((2 * HALO, cols), BF16),
            pltpu.VMEM((ITERS, peers, 2, cols), F32),
            pltpu.VMEM((ITERS, sizes[0], 2, cols), F32),
            pltpu.SemaphoreType.DMA((7,)),
            pltpu.SemaphoreType.DMA((2, 8)),
            pltpu.SemaphoreType.DMA((2, 8)),
            pltpu.SemaphoreType.DMA((2,)),
            pltpu.SemaphoreType.DMA((2, tiles)),
            pltpu.SemaphoreType.DMA((2, tiles)),
            pltpu.SemaphoreType.DMA((2, 2, ITERS)),
        ],
        compiler_params=pltpu.CompilerParams(collective_id=0, has_side_effects=True),
        name="fill_steps",
    )(*args)
    return x, y, z, weight[0, 0]


def solution(mesh):
    sizes = tuple(mesh.shape[axis] for axis in ("layer", "row", "col"))
    spec = P("layer", "row", "col")
    return jax.shard_map(
        functools.partial(local, sizes),
        mesh=mesh,
        in_specs=(spec,) * 7,
        out_specs=(spec, spec, spec, P()),
        check_vma=False,
    )
```

```python
import functools

import jax
import jax.numpy as jnp
from jax import lax
from jax.experimental import pallas as pl
from jax.experimental.pallas import tpu as pltpu
from jax.sharding import PartitionSpec as P

WIN = 50
CAP_LEVELS = 8
ITERS = 3

step_eta = 0.4
low_density = 0.35
high_density = 0.65
layer_gap = 0.15
tiny_term = 1e-06

HALF = WIN // 2
HALO = -(-HALF // 16) * 16
TILE = 128
MESH = pl.DeviceIdType.MESH
DIRS = ((-1, 0), (1, 0), (0, -1), (0, 1), (-1, -1), (-1, 1), (1, -1), (1, 1))
F32 = jnp.float32
BF16 = jnp.bfloat16
NT = (((1,), (1,)), ((), ()))
NN = (((1,), (0,)), ((), ()))


def split(value):
    high = value.astype(BF16)
    low = (value - high.astype(F32)).astype(BF16)
    return high, low


def dot(left, right, dims=NN):
    return lax.dot_general(left, right, dims, preferred_element_type=F32)


def iota(shape, dim):
    return lax.broadcasted_iota(jnp.int32, shape, dim)


def window(offset, start):
    return jnp.where((offset >= start) & (offset < start + WIN), 1.0, 0.0).astype(BF16)


def kernel(
    sizes, cost_in, dens_in, capc_in, blocked_in, x_in, y_in, z_in,
    x, y_out, z, weight_out,
    cost, dens, capc, blocked,
    ext_u, ext_y, et_u, et_y, ht_u, ht_y, above, below, zlow, cap, grad,
    band_r, band_h, band_c, pick, slots,
    load_sem, send_sem, recv_sem, first_sem, zsend, zrecv, sum_sem,
):
    nl, nr, nc = sizes
    layers, rows, cols = x_in.shape
    ndev = nl * nr * nc
    il, ir, ic = lax.axis_index("layer"), lax.axis_index("row"), lax.axis_index("col")
    me = (il * nr + ir) * nc + ic
    tiles = rows // TILE
    order = list(dict.fromkeys((0, tiles - 1, *range(tiles))))
    inverse_area = 1.0 / (WIN * WIN)
    own = pl.ds(HALO, rows)

    pairs = (
        (y_in, ext_y.at[:, own, :]), (x_in, x), (z_in, z), (cost_in, cost), (capc_in, capc),
        (blocked_in, blocked), (dens_in, dens),
    )
    loads = [pltpu.make_async_copy(a, b, load_sem.at[n]) for n, (a, b) in enumerate(pairs)]
    for load in loads:
        load.start()

    for ref in (ext_u, ext_y):
        ref[:, :HALO, :] = jnp.zeros((layers, HALO, cols), F32)
        ref[:, HALO + rows :, :] = jnp.zeros((layers, HALO, cols), F32)
    for ref in (ht_u, ht_y, above, below, zlow):
        ref[...] = jnp.zeros(ref.shape, F32)

    barrier = pltpu.get_barrier_semaphore()

    def others(act):
        def one(i, _):
            pl.when(i != me)(lambda: act((i // (nr * nc), (i // nc) % nr, i % nc)))
            return 0

        lax.fori_loop(0, ndev, one, 0, unroll=ndev <= 32)

    def greet(device):
        pl.semaphore_signal(barrier, inc=1, device_id=device, device_id_type=MESH)

    others(greet)

    keep_top = jnp.where(il < nl - 1, 1.0, 0.0).astype(F32)
    keep_low = jnp.where(il > 0, 1.0, 0.0).astype(F32)
    for which, start in ((0, -HALF), (1, 1 - HALF)):
        shape = (TILE, TILE + 2 * HALO)
        band_r[which] = window(iota(shape, 1) - HALO - iota(shape, 0), start)
        shape = (TILE, 3 * TILE)
        band_h[which] = window(iota(shape, 1) - TILE - iota(shape, 0), start)
        shape = (cols, cols)
        inner = window(iota(shape, 0) - iota(shape, 1), start)
        shape = (2 * HALO, cols)
        k = iota(shape, 0)
        place = jnp.where(k < HALO, k - HALO, k - HALO + cols)
        outer = window(place - iota(shape, 1), start)
        blank = jnp.zeros(shape, BF16)
        half = cols + layers * 2 * HALO
        for l in range(layers):
            for base in (0, half):
                band_c[which, l, base : base + cols] = inner
                for m in range(layers):
                    at = base + cols + m * 2 * HALO
                    band_c[which, l, at : at + 2 * HALO] = outer if m == l else blank
    shape = (2 * HALO, cols)
    k = iota(shape, 0)
    place = jnp.where(k < HALO, k, k - 2 * HALO + cols)
    pick[...] = jnp.where(place == iota(shape, 1), 1.0, 0.0).astype(BF16)

    def span(t, base=0):
        return pl.ds(t * TILE + base, TILE)

    def put_edges(et, l, t, value):
        et[l, :, span(t)] = dot(pick[...], value.astype(BF16), NT)

    loads[0].wait()
    for t in range(tiles):
        for l in range(layers):
            put_edges(et_y, l, t, ext_y[l, span(t, HALO), :])

    pl.semaphore_wait(barrier, ndev - 1)

    def copies(field):
        ext, et, ht = ((ext_u, et_u, ht_u), (ext_y, et_y, ht_y))[field]
        result = []
        for d, (dr, dc) in enumerate(DIRS):
            if dc == 0:
                src = ext.at[:, pl.ds(HALO if dr < 0 else rows, HALO), :]
                dst = ext.at[:, pl.ds(HALO + rows if dr < 0 else 0, HALO), :]
            else:
                from_rows = pl.ds(0 if dc < 0 else HALO, HALO)
                to_rows = pl.ds(HALO if dc < 0 else 0, HALO)
                if dr == 0:
                    src, dst = et.at[:, from_rows, :], ht.at[:, to_rows, pl.ds(TILE, rows)]
                elif dr < 0:
                    src = et.at[:, from_rows, pl.ds(0, TILE)]
                    dst = ht.at[:, to_rows, pl.ds(TILE + rows, TILE)]
                else:
                    src = et.at[:, from_rows, pl.ds(rows - TILE, TILE)]
                    dst = ht.at[:, to_rows, pl.ds(0, TILE)]
            to, frm = [], []
            if dr < 0:
                to.append(ir > 0)
                frm.append(ir < nr - 1)
            if dr > 0:
                to.append(ir < nr - 1)
                frm.append(ir > 0)
            if dc < 0:
                to.append(ic > 0)
                frm.append(ic < nc - 1)
            if dc > 0:
                to.append(ic < nc - 1)
                frm.append(ic > 0)
            copy = pltpu.make_async_remote_copy(
                src_ref=src, dst_ref=dst, send_sem=send_sem.at[field, d],
                recv_sem=recv_sem.at[field, d],
                device_id=(il, ir + dr, ic + dc), device_id_type=MESH,
            )
            result.append(
                (copy, functools.reduce(jnp.logical_and, to), functools.reduce(jnp.logical_and, frm))
            )
        return result

    halo_copies = (copies(0), copies(1))

    def begin(field, which):
        for d in which:
            copy, to, _ = halo_copies[field][d]
            pl.when(to)(copy.start)

    def finish(field):
        for copy, to, frm in halo_copies[field]:
            pl.when(frm)(copy.wait_recv)
            pl.when(to)(copy.wait_send)

    has_above, has_below = il < nl - 1, il > 0
    EDGE, SIDE = (4, 5, 6, 7, 0, 1), (2, 3)
    begin(1, EDGE + SIDE)
    first_up = pltpu.make_async_remote_copy(
        src_ref=z_in.at[layers - 1], dst_ref=zlow, send_sem=first_sem.at[0],
        recv_sem=first_sem.at[1], device_id=(il + 1, ir, ic), device_id_type=MESH,
    )
    pl.when(has_above)(first_up.start)

    def up(t):
        return pltpu.make_async_remote_copy(
            src_ref=ext_u.at[layers - 1, span(t, HALO), :], dst_ref=below.at[span(t), :],
            send_sem=zsend.at[0, t], recv_sem=zrecv.at[0, t],
            device_id=(il + 1, ir, ic), device_id_type=MESH,
        )

    def down(t):
        return pltpu.make_async_remote_copy(
            src_ref=ext_u.at[0, span(t, HALO), :], dst_ref=above.at[span(t), :],
            send_sem=zsend.at[1, t], recv_sem=zrecv.at[1, t],
            device_id=(il - 1, ir, ic), device_id_type=MESH,
        )

    def box(ext, ht, which, t):
        tall = pl.ds(t * TILE, TILE + 2 * HALO)
        wide = jnp.concatenate([ext[l, tall, :].astype(BF16) for l in range(layers)], axis=1)
        mid = dot(band_r[which], wide)
        halo = ht[:, :, t * TILE : (t + 3) * TILE].reshape(layers * 2 * HALO, 3 * TILE)
        side = dot(band_h[which], halo.astype(BF16), NT)
        result = []
        for l in range(layers):
            row = jnp.concatenate([mid[:, l * cols : (l + 1) * cols], side], axis=1)
            result.append(dot(jnp.concatenate(split(row), axis=1), band_c[which, l]))
        return result

    everywhere = [(l, t, (l, span(t), slice(None))) for t in order for l in range(layers)]
    for n in range(1, 7):
        loads[n].wait()
    z[layers - 1] = z[layers - 1] * keep_top
    for l, t, at in everywhere:
        level = (capc[at] + 1).astype(F32) * (1.0 / CAP_LEVELS)
        cap[at] = jnp.where(blocked[at] == 1, 0.0, level)

    def fold(value):
        return jnp.sum((value * value).reshape(TILE // 8, 8, cols), axis=0)

    def sums_begin(step, primal_sum, dual_sum):
        slots[step, pl.ds(me, 1)] = jnp.concatenate(
            [jnp.sum(primal_sum, axis=0, keepdims=True), jnp.sum(dual_sum, axis=0, keepdims=True)],
            axis=0,
        )[None]

        def send(device):
            pltpu.make_async_remote_copy(
                src_ref=slots.at[step, me], dst_ref=slots.at[step, me],
                send_sem=sum_sem.at[0, step], recv_sem=sum_sem.at[1, step],
                device_id=device, device_id_type=MESH,
            ).start()

        others(send)

    def sums_end(step, weight):
        some = slots.at[step, pl.ds(0, ndev - 1)]
        pltpu.make_async_copy(some, some, sum_sem.at[1, step]).wait()
        pltpu.make_async_copy(some, some, sum_sem.at[0, step]).wait()
        both = jnp.sum(slots[step], axis=0)
        primal = jnp.sum(both[0:1], axis=1, keepdims=True)
        dual = jnp.sum(both[1:2], axis=1, keepdims=True)
        ratio = jnp.broadcast_to((dual + tiny_term) / (primal + tiny_term), (1, cols))
        return jnp.sqrt(weight) * jnp.sqrt(jnp.sqrt(ratio))

    weight = jnp.ones((1, cols), F32)
    for step in range(ITERS):
        last = step == ITERS - 1
        if step == 0:
            pl.when(has_below)(first_up.wait_recv)
            pl.when(has_above)(first_up.wait_send)
        finish(1)
        for t in order:
            for l, area in enumerate(box(ext_y, ht_y, 1, t)):
                at = (l, span(t), slice(None))
                earlier = zlow[span(t), :] if l == 0 else z[l - 1, span(t), :]
                grad[at] = cost[at] + area * inverse_area + (z[at] - earlier)
        if step > 0:
            weight = sums_end(step - 1, weight)
        tau = step_eta / weight
        sigma = step_eta * weight
        sigma_inverse = 1.0 / sigma

        primal_sum = jnp.zeros((8, cols), F32)
        for l, t, at in everywhere:
            old = x[at]
            new = jnp.minimum(jnp.maximum(old - tau * grad[at], 0.0), cap[at])
            moved = new - old
            x[at] = new
            primal_sum = primal_sum + fold(moved)
            value = new + moved + dens[at]
            ext_u[l, span(t, HALO), :] = value
            put_edges(et_u, l, t, value)
            if l == layers - 1:
                if not last:
                    pl.when(has_above)(up(t).start)
                pl.when(has_below)(down(t).start)
                if t == order[min(1, tiles - 1)]:
                    begin(0, EDGE)
        begin(0, SIDE)
        finish(0)

        dual_sum = jnp.zeros((8, cols), F32)
        areas = {}
        for l, t, at in everywhere:
            if l == 0:
                areas = box(ext_u, ht_u, 0, t)
            old = ext_y[l, span(t, HALO), :]
            term = old * sigma_inverse + areas[l] * inverse_area
            capped = jnp.minimum(term, high_density)
            clipped = jnp.where(blocked[at] == 0, jnp.maximum(capped, low_density), capped)
            new = sigma * (term - clipped)
            dual_sum = dual_sum + fold(new - old)
            if last:
                y_out[at] = new
            else:
                ext_y[l, span(t, HALO), :] = new
                put_edges(et_y, l, t, new)
                if l == layers - 1 and t == order[min(1, tiles - 1)]:
                    begin(1, EDGE)
        if not last:
            begin(1, SIDE)

        def update(old, here, later, keep):
            term = old * sigma_inverse + keep * (here - later)
            return sigma * (term - jnp.clip(term, -layer_gap, layer_gap)) * keep

        for t in order:
            pl.when(has_above)(down(t).wait_recv)
            pl.when(has_below)(down(t).wait_send)
            if not last:
                pl.when(has_below)(up(t).wait_recv)
                pl.when(has_above)(up(t).wait_send)
            levels = [ext_u[l, span(t, HALO), :] for l in range(layers)] + [above[span(t), :]]
            for l in range(layers):
                at = (l, span(t), slice(None))
                old = z[at]
                new = update(old, levels[l], levels[l + 1], keep_top if l == layers - 1 else 1.0)
                z[at] = new
                dual_sum = dual_sum + fold(new - old)
            if not last:
                zlow[span(t), :] = update(zlow[span(t), :], below[span(t), :], levels[0], keep_low)
        sums_begin(step, primal_sum, dual_sum)

    weight_out[...] = sums_end(ITERS - 1, weight)


def local(sizes, *args):
    layers, rows, cols = args[0].shape
    ndev = sizes[0] * sizes[1] * sizes[2]
    tiles = rows // TILE
    whole = jax.ShapeDtypeStruct((layers, rows, cols), F32)
    vmem = pl.BlockSpec(memory_space=pltpu.VMEM)
    anywhere = pl.BlockSpec(memory_space=pl.ANY)
    full = pltpu.VMEM((layers, rows, cols), F32)
    full_int = pltpu.VMEM((layers, rows, cols), jnp.int32)
    line = pltpu.VMEM((1, cols), F32)
    ext = pltpu.VMEM((layers, rows + 2 * HALO, cols), F32)
    et = pltpu.VMEM((layers, 2 * HALO, rows), F32)
    ht = pltpu.VMEM((layers, 2 * HALO, rows + 2 * TILE), F32)
    plane = pltpu.VMEM((rows, cols), F32)
    x, y, z, weight = pl.pallas_call(
        functools.partial(kernel, sizes),
        out_shape=(full, full, full, line),
        in_specs=[anywhere] * 7,
        out_specs=(vmem,) * 4,
        scratch_shapes=[
            full, full, full_int, full_int,
            ext, ext, et, et, ht, ht, plane, plane, plane, full, full,
            pltpu.VMEM((2, TILE, TILE + 2 * HALO), BF16),
            pltpu.VMEM((2, TILE, 3 * TILE), BF16),
            pltpu.VMEM((2, layers, 2 * (cols + layers * 2 * HALO), cols), BF16),
            pltpu.VMEM((2 * HALO, cols), BF16),
            pltpu.VMEM((ITERS, ndev, 2, cols), F32),
            pltpu.SemaphoreType.DMA((7,)),
            pltpu.SemaphoreType.DMA((2, 8)),
            pltpu.SemaphoreType.DMA((2, 8)),
            pltpu.SemaphoreType.DMA((2,)),
            pltpu.SemaphoreType.DMA((2, tiles)),
            pltpu.SemaphoreType.DMA((2, tiles)),
            pltpu.SemaphoreType.DMA((2, ITERS)),
        ],
        compiler_params=pltpu.CompilerParams(collective_id=0, has_side_effects=True),
        name="fill_steps",
    )(*args)
    return x, y, z, weight[0, 0]


def solution(mesh):
    sizes = tuple(mesh.shape[axis] for axis in ("layer", "row", "col"))
    spec = P("layer", "row", "col")
    return jax.shard_map(
        functools.partial(local, sizes),
        mesh=mesh,
        in_specs=(spec,) * 7,
        out_specs=(spec, spec, spec, P()),
        check_vma=False,
    )
```

```python
import functools

import jax
import jax.numpy as jnp
from jax import lax
from jax.experimental import pallas as pl
from jax.experimental.pallas import tpu as pltpu
from jax.sharding import PartitionSpec as P

WIN = 50
CAP_LEVELS = 8
ITERS = 3

step_eta = 0.4
low_density = 0.35
high_density = 0.65
layer_gap = 0.15
tiny_term = 1e-06

HALF = WIN // 2
HALO = -(-HALF // 16) * 16
TILE = 128
MESH = pl.DeviceIdType.MESH
DIRS = ((-1, 0), (1, 0), (0, -1), (0, 1), (-1, -1), (-1, 1), (1, -1), (1, 1))
F32 = jnp.float32
BF16 = jnp.bfloat16
NT = (((1,), (1,)), ((), ()))
NN = (((1,), (0,)), ((), ()))


def split(value):
    high = value.astype(BF16)
    low = (value - high.astype(F32)).astype(BF16)
    return high, low


def dot(left, right, dims=NN):
    return lax.dot_general(left, right, dims, preferred_element_type=F32)


def iota(shape, dim):
    return lax.broadcasted_iota(jnp.int32, shape, dim)


def window(offset, start):
    return jnp.where((offset >= start) & (offset < start + WIN), 1.0, 0.0).astype(BF16)


def kernel(
    sizes, cost_in, dens_in, capc_in, blocked_in, x_in, y_in, z_in,
    x, y_out, z, weight_out,
    cost, dens, capc, blocked,
    ext_u, ext_y, et_u, et_y, ht_u, ht_y, above, below, zlow, cap, grad,
    band_r, band_h, band_c, pick, slots,
    load_sem, send_sem, recv_sem, first_sem, zsend, zrecv, sum_sem, zhigh, tsend, trecv,
):
    nl, nr, nc = sizes
    layers, rows, cols = x_in.shape
    ndev = nl * nr * nc
    il, ir, ic = lax.axis_index("layer"), lax.axis_index("row"), lax.axis_index("col")
    me = (il * nr + ir) * nc + ic
    tiles = rows // TILE
    order = list(dict.fromkeys((0, tiles - 1, *range(tiles))))
    inverse_area = 1.0 / (WIN * WIN)
    own = pl.ds(HALO, rows)

    pairs = (
        (y_in, ext_y.at[:, own, :]), (x_in, x), (z_in, z), (cost_in, cost), (capc_in, capc),
        (blocked_in, blocked), (dens_in, dens),
    )
    loads = [pltpu.make_async_copy(a, b, load_sem.at[n]) for n, (a, b) in enumerate(pairs)]
    for load in loads:
        load.start()

    for ref in (ext_u, ext_y):
        ref[:, :HALO, :] = jnp.zeros((layers, HALO, cols), F32)
        ref[:, HALO + rows :, :] = jnp.zeros((layers, HALO, cols), F32)
    for ref in (ht_u, ht_y, above, below, zlow, zhigh):
        ref[...] = jnp.zeros(ref.shape, F32)

    barrier = pltpu.get_barrier_semaphore()

    def others(act):
        def one(i, _):
            pl.when(i != me)(lambda: act((i // (nr * nc), (i // nc) % nr, i % nc)))
            return 0

        lax.fori_loop(0, ndev, one, 0, unroll=ndev <= 32)

    def greet(device):
        pl.semaphore_signal(barrier, inc=1, device_id=device, device_id_type=MESH)

    others(greet)

    keep_top = jnp.where(il < nl - 1, 1.0, 0.0).astype(F32)
    keep_low = jnp.where(il > 0, 1.0, 0.0).astype(F32)
    for which, start in ((0, -HALF), (1, 1 - HALF)):
        shape = (TILE, TILE + 2 * HALO)
        band_r[which] = window(iota(shape, 1) - HALO - iota(shape, 0), start)
        shape = (TILE, 3 * TILE)
        band_h[which] = window(iota(shape, 1) - TILE - iota(shape, 0), start)
        shape = (cols, cols)
        inner = window(iota(shape, 0) - iota(shape, 1), start)
        shape = (2 * HALO, cols)
        k = iota(shape, 0)
        place = jnp.where(k < HALO, k - HALO, k - HALO + cols)
        outer = window(place - iota(shape, 1), start)
        blank = jnp.zeros(shape, BF16)
        half = cols + layers * 2 * HALO
        for l in range(layers):
            for base in (0, half):
                band_c[which, l, base : base + cols] = inner
                for m in range(layers):
                    at = base + cols + m * 2 * HALO
                    band_c[which, l, at : at + 2 * HALO] = outer if m == l else blank
    shape = (2 * HALO, cols)
    k = iota(shape, 0)
    place = jnp.where(k < HALO, k, k - 2 * HALO + cols)
    pick[...] = jnp.where(place == iota(shape, 1), 1.0, 0.0).astype(BF16)

    def span(t, base=0):
        return pl.ds(t * TILE + base, TILE)

    def put_edges(et, l, t, value):
        et[l, :, span(t)] = dot(pick[...], value.astype(BF16), NT)

    loads[0].wait()
    for t in range(tiles):
        for l in range(layers):
            put_edges(et_y, l, t, ext_y[l, span(t, HALO), :])

    pl.semaphore_wait(barrier, ndev - 1)

    def copies(field):
        ext, et, ht = ((ext_u, et_u, ht_u), (ext_y, et_y, ht_y))[field]
        result = []
        for d, (dr, dc) in enumerate(DIRS):
            if dc == 0:
                src = ext.at[:, pl.ds(HALO if dr < 0 else rows, HALO), :]
                dst = ext.at[:, pl.ds(HALO + rows if dr < 0 else 0, HALO), :]
            else:
                from_rows = pl.ds(0 if dc < 0 else HALO, HALO)
                to_rows = pl.ds(HALO if dc < 0 else 0, HALO)
                if dr == 0:
                    src, dst = et.at[:, from_rows, :], ht.at[:, to_rows, pl.ds(TILE, rows)]
                elif dr < 0:
                    src = et.at[:, from_rows, pl.ds(0, TILE)]
                    dst = ht.at[:, to_rows, pl.ds(TILE + rows, TILE)]
                else:
                    src = et.at[:, from_rows, pl.ds(rows - TILE, TILE)]
                    dst = ht.at[:, to_rows, pl.ds(0, TILE)]
            to, frm = [], []
            if dr < 0:
                to.append(ir > 0)
                frm.append(ir < nr - 1)
            if dr > 0:
                to.append(ir < nr - 1)
                frm.append(ir > 0)
            if dc < 0:
                to.append(ic > 0)
                frm.append(ic < nc - 1)
            if dc > 0:
                to.append(ic < nc - 1)
                frm.append(ic > 0)
            copy = pltpu.make_async_remote_copy(
                src_ref=src, dst_ref=dst, send_sem=send_sem.at[field, d],
                recv_sem=recv_sem.at[field, d],
                device_id=(il, ir + dr, ic + dc), device_id_type=MESH,
            )
            result.append(
                (copy, functools.reduce(jnp.logical_and, to), functools.reduce(jnp.logical_and, frm))
            )
        return result

    halo_copies = (copies(0), copies(1))

    def begin(field, which):
        for d in which:
            copy, to, _ = halo_copies[field][d]
            pl.when(to)(copy.start)

    def finish(field):
        for copy, to, frm in halo_copies[field]:
            pl.when(frm)(copy.wait_recv)
            pl.when(to)(copy.wait_send)

    has_above, has_below = il < nl - 1, il > 0
    EDGE, SIDE = (4, 5, 6, 7, 0, 1), (2, 3)
    begin(1, EDGE + SIDE)
    first_up = pltpu.make_async_remote_copy(
        src_ref=z_in.at[layers - 1], dst_ref=zlow, send_sem=first_sem.at[0],
        recv_sem=first_sem.at[1], device_id=(il + 1, ir, ic), device_id_type=MESH,
    )
    pl.when(has_above)(first_up.start)

    def up(t):
        return pltpu.make_async_remote_copy(
            src_ref=ext_u.at[layers - 1, span(t, HALO), :], dst_ref=below.at[span(t), :],
            send_sem=zsend.at[0, t], recv_sem=zrecv.at[0, t],
            device_id=(il + 1, ir, ic), device_id_type=MESH,
        )

    def down(t):
        return pltpu.make_async_remote_copy(
            src_ref=ext_u.at[0, span(t, HALO), :], dst_ref=above.at[span(t), :],
            send_sem=zsend.at[1, t], recv_sem=zrecv.at[1, t],
            device_id=(il - 1, ir, ic), device_id_type=MESH,
        )

    lower, upper = order[0::2], order[1::2]

    def give_up(t):
        return pltpu.make_async_remote_copy(
            src_ref=z.at[layers - 1, span(t), :], dst_ref=zlow.at[span(t), :],
            send_sem=tsend.at[t], recv_sem=trecv.at[t],
            device_id=(il + 1, ir, ic), device_id_type=MESH,
        )

    def give_down(t):
        return pltpu.make_async_remote_copy(
            src_ref=zlow.at[span(t), :], dst_ref=zhigh.at[span(t), :],
            send_sem=tsend.at[t], recv_sem=trecv.at[t],
            device_id=(il - 1, ir, ic), device_id_type=MESH,
        )

    def take(last):
        for t in upper:
            pl.when(has_above)(give_down(t).wait_recv)
            pl.when(has_below)(give_down(t).wait_send)
            z[layers - 1, span(t), :] = zhigh[span(t), :]
        if not last:
            for t in lower:
                pl.when(has_below)(give_up(t).wait_recv)
                pl.when(has_above)(give_up(t).wait_send)

    def box(ext, ht, which, t):
        tall = pl.ds(t * TILE, TILE + 2 * HALO)
        wide = jnp.concatenate([ext[l, tall, :].astype(BF16) for l in range(layers)], axis=1)
        mid = dot(band_r[which], wide)
        halo = ht[:, :, t * TILE : (t + 3) * TILE].reshape(layers * 2 * HALO, 3 * TILE)
        side = dot(band_h[which], halo.astype(BF16), NT)
        result = []
        for l in range(layers):
            row = jnp.concatenate([mid[:, l * cols : (l + 1) * cols], side], axis=1)
            result.append(dot(jnp.concatenate(split(row), axis=1), band_c[which, l]))
        return result

    everywhere = [(l, t, (l, span(t), slice(None))) for t in order for l in range(layers)]
    for n in range(1, 7):
        loads[n].wait()
    z[layers - 1] = z[layers - 1] * keep_top
    for l, t, at in everywhere:
        level = (capc[at] + 1).astype(F32) * (1.0 / CAP_LEVELS)
        cap[at] = jnp.where(blocked[at] == 1, 0.0, level)

    def fold(value):
        return jnp.sum((value * value).reshape(TILE // 8, 8, cols), axis=0)

    def sums_begin(step, primal_sum, dual_sum):
        slots[step, pl.ds(me, 1)] = jnp.concatenate(
            [jnp.sum(primal_sum, axis=0, keepdims=True), jnp.sum(dual_sum, axis=0, keepdims=True)],
            axis=0,
        )[None]

        def send(device):
            pltpu.make_async_remote_copy(
                src_ref=slots.at[step, me], dst_ref=slots.at[step, me],
                send_sem=sum_sem.at[0, step], recv_sem=sum_sem.at[1, step],
                device_id=device, device_id_type=MESH,
            ).start()

        others(send)

    def sums_end(step, weight):
        some = slots.at[step, pl.ds(0, ndev - 1)]
        pltpu.make_async_copy(some, some, sum_sem.at[1, step]).wait()
        pltpu.make_async_copy(some, some, sum_sem.at[0, step]).wait()
        both = jnp.sum(slots[step], axis=0)
        primal = jnp.sum(both[0:1], axis=1, keepdims=True)
        dual = jnp.sum(both[1:2], axis=1, keepdims=True)
        ratio = jnp.broadcast_to((dual + tiny_term) / (primal + tiny_term), (1, cols))
        return jnp.sqrt(weight) * jnp.sqrt(jnp.sqrt(ratio))

    weight = jnp.ones((1, cols), F32)
    for step in range(ITERS):
        last = step == ITERS - 1
        if step == 0:
            pl.when(has_below)(first_up.wait_recv)
            pl.when(has_above)(first_up.wait_send)
        finish(1)
        if step > 0:
            take(False)
        for t in order:
            for l, area in enumerate(box(ext_y, ht_y, 1, t)):
                at = (l, span(t), slice(None))
                earlier = zlow[span(t), :] if l == 0 else z[l - 1, span(t), :]
                grad[at] = cost[at] + area * inverse_area + (z[at] - earlier)
        if step > 0:
            weight = sums_end(step - 1, weight)
        tau = step_eta / weight
        sigma = step_eta * weight
        sigma_inverse = 1.0 / sigma

        primal_sum = jnp.zeros((8, cols), F32)
        for l, t, at in everywhere:
            old = x[at]
            new = jnp.minimum(jnp.maximum(old - tau * grad[at], 0.0), cap[at])
            moved = new - old
            x[at] = new
            primal_sum = primal_sum + fold(moved)
            value = new + moved + dens[at]
            ext_u[l, span(t, HALO), :] = value
            put_edges(et_u, l, t, value)
            if l == layers - 1:
                if t in upper:
                    pl.when(has_above)(up(t).start)
                else:
                    pl.when(has_below)(down(t).start)
                if t == order[min(1, tiles - 1)]:
                    begin(0, EDGE)
        begin(0, SIDE)
        finish(0)

        dual_sum = jnp.zeros((8, cols), F32)
        areas = {}
        for l, t, at in everywhere:
            if l == 0:
                areas = box(ext_u, ht_u, 0, t)
            old = ext_y[l, span(t, HALO), :]
            term = old * sigma_inverse + areas[l] * inverse_area
            capped = jnp.minimum(term, high_density)
            clipped = jnp.where(blocked[at] == 0, jnp.maximum(capped, low_density), capped)
            new = sigma * (term - clipped)
            dual_sum = dual_sum + fold(new - old)
            if last:
                y_out[at] = new
            else:
                ext_y[l, span(t, HALO), :] = new
                put_edges(et_y, l, t, new)
                if l == layers - 1 and t == order[min(1, tiles - 1)]:
                    begin(1, EDGE)
        if not last:
            begin(1, SIDE)

        def update(old, here, later, keep):
            term = old * sigma_inverse + keep * (here - later)
            return sigma * (term - jnp.clip(term, -layer_gap, layer_gap)) * keep

        for t in order:
            levels = [ext_u[l, span(t, HALO), :] for l in range(layers)]
            for l in range(layers - 1):
                at = (l, span(t), slice(None))
                old = z[at]
                new = update(old, levels[l], levels[l + 1], 1.0)
                z[at] = new
                dual_sum = dual_sum + fold(new - old)
            if t in lower:
                pl.when(has_above)(down(t).wait_recv)
                pl.when(has_below)(down(t).wait_send)
                old = z[layers - 1, span(t), :]
                new = update(old, levels[layers - 1], above[span(t), :], keep_top)
                z[layers - 1, span(t), :] = new
            else:
                pl.when(has_below)(up(t).wait_recv)
                pl.when(has_above)(up(t).wait_send)
                old = zlow[span(t), :]
                new = update(old, below[span(t), :], levels[0], keep_low)
                zlow[span(t), :] = new
            dual_sum = dual_sum + fold(new - old)
        sums_begin(step, primal_sum, dual_sum)
        for t in order:
            if t in upper:
                pl.when(has_below)(give_down(t).start)
            elif not last:
                pl.when(has_above)(give_up(t).start)

    take(True)
    weight_out[...] = sums_end(ITERS - 1, weight)


def local(sizes, *args):
    layers, rows, cols = args[0].shape
    ndev = sizes[0] * sizes[1] * sizes[2]
    tiles = rows // TILE
    whole = jax.ShapeDtypeStruct((layers, rows, cols), F32)
    vmem = pl.BlockSpec(memory_space=pltpu.VMEM)
    anywhere = pl.BlockSpec(memory_space=pl.ANY)
    full = pltpu.VMEM((layers, rows, cols), F32)
    full_int = pltpu.VMEM((layers, rows, cols), jnp.int32)
    line = pltpu.VMEM((1, cols), F32)
    ext = pltpu.VMEM((layers, rows + 2 * HALO, cols), F32)
    et = pltpu.VMEM((layers, 2 * HALO, rows), F32)
    ht = pltpu.VMEM((layers, 2 * HALO, rows + 2 * TILE), F32)
    plane = pltpu.VMEM((rows, cols), F32)
    x, y, z, weight = pl.pallas_call(
        functools.partial(kernel, sizes),
        out_shape=(full, full, full, line),
        in_specs=[anywhere] * 7,
        out_specs=(vmem,) * 4,
        scratch_shapes=[
            full, full, full_int, full_int,
            ext, ext, et, et, ht, ht, plane, plane, plane, full, full,
            pltpu.VMEM((2, TILE, TILE + 2 * HALO), BF16),
            pltpu.VMEM((2, TILE, 3 * TILE), BF16),
            pltpu.VMEM((2, layers, 2 * (cols + layers * 2 * HALO), cols), BF16),
            pltpu.VMEM((2 * HALO, cols), BF16),
            pltpu.VMEM((ITERS, ndev, 2, cols), F32),
            pltpu.SemaphoreType.DMA((7,)),
            pltpu.SemaphoreType.DMA((2, 8)),
            pltpu.SemaphoreType.DMA((2, 8)),
            pltpu.SemaphoreType.DMA((2,)),
            pltpu.SemaphoreType.DMA((2, tiles)),
            pltpu.SemaphoreType.DMA((2, tiles)),
            pltpu.SemaphoreType.DMA((2, ITERS)),
            plane,
            pltpu.SemaphoreType.DMA((tiles,)),
            pltpu.SemaphoreType.DMA((tiles,)),
        ],
        compiler_params=pltpu.CompilerParams(collective_id=0, has_side_effects=True),
        name="fill_steps",
    )(*args)
    return x, y, z, weight[0, 0]


def solution(mesh):
    sizes = tuple(mesh.shape[axis] for axis in ("layer", "row", "col"))
    spec = P("layer", "row", "col")
    return jax.shard_map(
        functools.partial(local, sizes),
        mesh=mesh,
        in_specs=(spec,) * 7,
        out_specs=(spec, spec, spec, P()),
        check_vma=False,
    )
```
